768 devices in a mesh: section: 48 (over x, z_lo, core), head: 16 (over y, z_hi).
Axes of the slice: x: 4, y: 8, z: 12 (z_hi: 2, z_lo: 6; z = z_hi * 6 + z_lo), core: 2. Of those that a mesh axis runs over, the one named last changes fastest.
Arguments:
- residual: bfloat16 [12288, 2, 4096], P(('section', 'head')), may hold values from -3 to 3
- queries: bfloat16 [2, 12288, 4096], P(None, 'section', 'head'), may hold values from -80 to 80
- new_kv: bfloat16 [2, 2, 12288, 1024], P(None, None, 'section'), may hold values from -6 to 6
- cache_kv: bfloat16 [2, 73728, 1024], P(None, 'section'), may hold values from -6 to 6
- lengths: int32 [48], replicated, may hold values from 1 to 1536, as said below
- out_weight: bfloat16 [48, 4096, 4096], P('section', 'head'), may hold values from -0.09375 to 0.09375
Outputs:
- advanced: bfloat16 [12288, 2, 4096], P(('section', 'head'))
The draws below stay inside these ranges and needn't reach their ends.
Inputs may be any that keep to these rules, and one draw needn't show every extreme that they name: `lengths`: some section's cache holds 1536 positions while the section half the sections away holds at most 128.
All inputs are finite; a program needn't handle non-finite values.
Results may differ from the reference program's by a relative error of at most 0.013.
Values may be sent and summed in bfloat16 or wider, within the bound.
A program may use at most 64 MiB of HBM per device.

```python
import math
import jax
import jax.numpy as jnp
from jax import lax

D = 4096
QH = 32
KVH = 8
HD = 128
ROWS = 256
BLK = 128
TICKS = 2
SECTIONS = 48
TOKENS = 12288
CMAX = 1536
N_HEAD = 16


def draw_queries(key, part):
    first_key = jax.random.fold_in(key, 11)
    shape_now = (TICKS, SECTIONS, ROWS, QH * HD)
    values = jnp.clip(jax.random.normal(first_key, shape_now, jnp.float32), -5.0, 5.0)
    return values.reshape(TICKS, TOKENS, QH * HD).astype(jnp.bfloat16)


def draw_new_kv(key, part):
    first_key = jax.random.fold_in(key, 21)
    shape_now = (TICKS, 2, SECTIONS, ROWS, KVH * HD)
    values = jnp.clip(jax.random.normal(first_key, shape_now, jnp.float32), -5.0, 5.0)
    return values.reshape(TICKS, 2, TOKENS, KVH * HD).astype(jnp.bfloat16)


def draw_cache_kv(key, part):
    first_key = jax.random.fold_in(key, 31)
    shape_now = (2, SECTIONS, CMAX, KVH * HD)
    values = jnp.clip(jax.random.normal(first_key, shape_now, jnp.float32), -5.0, 5.0)
    return values.reshape(2, SECTIONS * CMAX, KVH * HD).astype(jnp.bfloat16)


def draw_lengths(key, part):
    first_draw = jax.random.randint(jax.random.fold_in(key, 41), (SECTIONS,), 1, CMAX + 1)
    second_draw = jax.random.randint(jax.random.fold_in(key, 42), (SECTIONS,), 1, CMAX + 1)
    lengths = jnp.minimum(first_draw, second_draw).astype(jnp.int32)
    chosen = jax.random.randint(jax.random.fold_in(key, 43), (), 0, SECTIONS // 2)
    short_length = jax.random.randint(jax.random.fold_in(key, 44), (), 1, BLK + 1)
    section_ids = jnp.arange(SECTIONS, dtype=jnp.int32)
    lengths = jnp.where(section_ids == chosen, CMAX, lengths)
    lengths = jnp.where(section_ids == chosen + SECTIONS // 2, short_length, lengths)
    return lengths.astype(jnp.int32)


def block_levels(stream_key, shape, shards, low, top_value):
    level = 1.0
    for position, blocks in shards:
        steps = jax.random.uniform(jax.random.fold_in(jax.random.fold_in(stream_key, 6), position), (blocks,), jnp.float32, low / len(shards), top_value / len(shards))
        level = level * jnp.repeat(jnp.exp(steps), shape[position] // blocks).reshape((-1,) + (1,) * (len(shape) - 1 - position))
    return level


def normal_values(key, dims, spread, reach, split=(), kind=jnp.bfloat16):
    entries = jax.random.normal(key, dims, jnp.float32) * spread
    if len(split) > 0:
        entries = block_levels(key, dims, split, -0.22, 0.18) * entries
    return jnp.clip(entries, min=-reach, max=reach).astype(kind)


def setup_inputs(seed: int = 0) -> dict:
    key_of = jax.random.split(jax.random.key(seed), 7)
    residual = normal_values(key_of[0], (TOKENS, TICKS, D), 0.5, 3.0, ((0, 768),))
    queries = draw_queries(jax.random.fold_in(key_of[6], 71), 0)
    new_kv = draw_new_kv(jax.random.fold_in(key_of[6], 71), 0)
    cache_kv = draw_cache_kv(jax.random.fold_in(key_of[6], 71), 0)
    lengths = draw_lengths(jax.random.fold_in(key_of[6], 71), 0)
    out_weight = normal_values(key_of[5], (SECTIONS, QH * HD, D), (QH * HD) ** -0.5, 0.09375, ((0, 48), (1, 16)))
    return dict(residual=residual, queries=queries, new_kv=new_kv, cache_kv=cache_kv, lengths=lengths, out_weight=out_weight)


def section_heads(query_now, fresh_now, cache_now, length_now):
    group_size = QH // KVH
    key_count = CMAX + TICKS * ROWS
    key_rows = jnp.concatenate([cache_now[0]] + [fresh_now[earlier, 0] for earlier in range(TICKS)], axis=0)
    value_rows = jnp.concatenate([cache_now[1]] + [fresh_now[earlier, 1] for earlier in range(TICKS)], axis=0)
    key_rows = key_rows.astype(jnp.float32).reshape(key_count, KVH, HD)
    value_rows = value_rows.astype(jnp.float32).reshape(key_count, KVH, HD)
    key_slot = jnp.arange(key_count)
    in_cache = key_slot < CMAX
    cache_used = key_slot < length_now
    fresh_tick = (key_slot - CMAX) // ROWS
    fresh_row = (key_slot - CMAX) % ROWS
    row_index = jnp.arange(ROWS)
    results = []
    for tick_now in range(TICKS):
        later = (fresh_tick[None, :] < tick_now) | (fresh_tick[None, :] == tick_now) & (fresh_row[None, :] <= row_index[:, None])
        visible = jnp.where(in_cache[None, :], cache_used[None, :], later)
        query_rows = query_now[tick_now].astype(jnp.float32).reshape(ROWS, KVH, group_size, HD)
        scores = jnp.einsum('rkgd,lkd->kgrl', query_rows, key_rows, precision=lax.Precision.HIGHEST) / math.sqrt(HD)
        scores = jnp.where(visible[None, None], scores, -1e+30)
        highest = lax.optimization_barrier(jnp.max(scores, axis=-1, keepdims=True))
        weights = jnp.where(visible[None, None], jnp.exp(scores - highest), 0.0)
        totals = lax.optimization_barrier(jnp.sum(weights, axis=-1))
        rounded = lax.optimization_barrier(weights.astype(jnp.bfloat16)).astype(jnp.float32)
        mixed = jnp.einsum('kgrl,lkd->rkgd', rounded, value_rows, precision=lax.Precision.HIGHEST)
        mixed = mixed / totals.transpose(2, 0, 1)[..., None]
        results.append(mixed.reshape(ROWS, QH * HD).astype(jnp.bfloat16))
    return jnp.stack(results)

def section_update(heads_now, weight_now, rows_now):
    group_heads = QH // N_HEAD
    parts = heads_now.astype(jnp.float32).reshape(TICKS, ROWS, N_HEAD, group_heads * HD)
    weight_parts = weight_now.astype(jnp.float32).reshape(N_HEAD, group_heads * HD, D)
    results = []
    for tick_now in range(TICKS):
        partial_sums = jnp.einsum('rgk,gkd->grd', parts[tick_now], weight_parts, precision=lax.Precision.HIGHEST)
        rounded = lax.optimization_barrier(partial_sums.astype(jnp.bfloat16)).astype(jnp.float32)
        projected = lax.optimization_barrier(jnp.sum(rounded, axis=0))
        results.append((rows_now[:, tick_now].astype(jnp.float32) + projected).astype(jnp.bfloat16))
    return jnp.stack(results, axis=1)

def reference(residual, queries, new_kv, cache_kv, lengths, out_weight):
    query_sections = queries.reshape(TICKS, SECTIONS, ROWS, QH * HD).transpose(1, 0, 2, 3)
    fresh_sections = new_kv.reshape(TICKS, 2, SECTIONS, ROWS, KVH * HD).transpose(2, 0, 1, 3, 4)
    cache_sections = cache_kv.reshape(2, SECTIONS, CMAX, KVH * HD).transpose(1, 0, 2, 3)
    residual_sections = residual.reshape(SECTIONS, ROWS, TICKS, D)

    def per_section(items):
        query_now, fresh_now, cache_now, length_now, weight_now, rows_now = items
        heads_now = section_heads(query_now, fresh_now, cache_now, length_now)
        return section_update(heads_now, weight_now, rows_now)
    updated = lax.map(per_section, (query_sections, fresh_sections, cache_sections, lengths, out_weight, residual_sections))
    advanced = jnp.roll(updated, 1, axis=0)
    return advanced.reshape(TOKENS, TICKS, D)
```

```python
import functools
import math

import jax
import jax.numpy as jnp
from jax import lax
from jax.experimental import pallas as pl
from jax.experimental.pallas import tpu as pltpu
from jax.sharding import PartitionSpec as P

HD = 128
KBLK = 512
NEG = -1e30
SCALE = math.log2(math.e) / math.sqrt(HD)
SPLIT = 2
SKEW = (0, 1, 4, 5)
MESH = pl.DeviceIdType.MESH


def attend_kernel(
    len_ref, q_ref, new_ref, cache_ref, o_ref, fresh, cache, m_ref, l_ref, acc_ref, fsem, csem
):
    ticks, rows, width = q_ref.shape
    here = width // HD
    key_blocks = cache.shape[0]
    length = len_ref[lax.axis_index("section")]
    column = pl.multiple_of((lax.axis_index("head") // 2) * HD, HD)
    used = (length + KBLK - 1) // KBLK

    def fresh_copy(t, i):
        return pltpu.make_async_copy(
            new_ref.at[t, i, :, pl.ds(column, HD)],
            fresh.at[i, pl.ds(t * rows, rows), :],
            fsem.at[t, i],
        )

    def cache_copy(b, i):
        return pltpu.make_async_copy(
            cache_ref.at[i, pl.ds(b * KBLK, KBLK), pl.ds(column, HD)],
            cache.at[b, i],
            csem.at[b, i],
        )

    for t in range(ticks):
        for i in range(2):
            fresh_copy(t, i).start()
    for b in range(key_blocks):
        @pl.when(b < used)
        def _(b=b):
            for i in range(2):
                cache_copy(b, i).start()
    for t in range(ticks):
        for i in range(2):
            fresh_copy(t, i).wait()

    def scores_of(t, h, keys):
        q = q_ref[t, :, h * HD:(h + 1) * HD]
        return lax.dot_general(
            q, keys, (((1,), (1,)), ((), ())), preferred_element_type=jnp.float32
        )

    for t in range(ticks):
        count = (t + 1) * rows
        row_id = lax.broadcasted_iota(jnp.int32, (rows, count), 0)
        col_id = lax.broadcasted_iota(jnp.int32, (rows, count), 1)
        seen = col_id <= row_id + t * rows
        for h in range(here):
            at = t * here + h
            s = jnp.where(seen, scores_of(t, h, fresh[0, 0:count, :]), NEG)
            m = jnp.max(s, axis=1, keepdims=True)
            p = jnp.exp2((s - m) * SCALE)
            m_ref[at] = m
            l_ref[at] = jnp.sum(p, axis=1, keepdims=True)
            acc_ref[at] = jnp.dot(
                p.astype(jnp.bfloat16), fresh[1, 0:count, :], preferred_element_type=jnp.float32
            )

    def one_block(b, carry):
        for i in range(2):
            cache_copy(b, i).wait()
        col_id = lax.broadcasted_iota(jnp.int32, (1, KBLK), 1) + b * KBLK
        seen = col_id < length
        keys = cache[b, 0]
        values = cache[b, 1]
        for t in range(ticks):
            for h in range(here):
                at = t * here + h
                s = jnp.where(seen, scores_of(t, h, keys), NEG)
                before = m_ref[at]
                m = jnp.maximum(before, jnp.max(s, axis=1, keepdims=True))
                p = jnp.exp2((s - m) * SCALE)
                factor = jnp.exp2((before - m) * SCALE)
                m_ref[at] = m
                l_ref[at] = l_ref[at] * factor + jnp.sum(p, axis=1, keepdims=True)
                acc_ref[at] = acc_ref[at] * factor + jnp.dot(
                    p.astype(jnp.bfloat16), values, preferred_element_type=jnp.float32
                )
        return carry

    lax.fori_loop(0, used, one_block, 0)
    for t in range(ticks):
        for h in range(here):
            at = t * here + h
            o_ref[t, :, h * HD:(h + 1) * HD] = (acc_ref[at] / l_ref[at]).astype(jnp.bfloat16)


def attend(queries, new_kv, cache_kv, lengths):
    ticks, rows, width = queries.shape
    here = width // HD
    capacity = cache_kv.shape[1]
    return pl.pallas_call(
        attend_kernel,
        out_shape=jax.ShapeDtypeStruct(queries.shape, jnp.bfloat16),
        in_specs=[
            pl.BlockSpec(memory_space=pltpu.SMEM),
            pl.BlockSpec(memory_space=pltpu.VMEM),
            pl.BlockSpec(memory_space=pl.ANY),
            pl.BlockSpec(memory_space=pl.ANY),
        ],
        out_specs=pl.BlockSpec(memory_space=pltpu.VMEM),
        scratch_shapes=[
            pltpu.VMEM((2, ticks * rows, HD), jnp.bfloat16),
            pltpu.VMEM((capacity // KBLK, 2, KBLK, HD), jnp.bfloat16),
            pltpu.VMEM((ticks * here, rows, 1), jnp.float32),
            pltpu.VMEM((ticks * here, rows, 1), jnp.float32),
            pltpu.VMEM((ticks * here, rows, HD), jnp.float32),
            pltpu.SemaphoreType.DMA((ticks, 2)),
            pltpu.SemaphoreType.DMA((capacity // KBLK, 2)),
        ],
        name="attend",
    )(lengths, queries, new_kv, cache_kv)


def reduce_kernel(
    sections,
    heads_count,
    heads_ref,
    w_ref,
    res_ref,
    land_ref,
    res_land,
    part,
    buf,
    ssem,
    rsem,
    zssem,
    zrsem,
    xsem,
):
    ny = heads_count // 2
    hops = ny - 1
    groups = buf.shape[2]
    ticks = heads_ref.shape[0]
    chunk = buf.shape[3]
    wide = buf.shape[4]
    own = chunk // 2
    half = w_ref.shape[1] // 2
    section = lax.axis_index("section")
    head = lax.axis_index("head")
    y = head // 2
    z = head % 2
    after = lax.rem(section + 1, sections)
    prior = lax.rem(section + sections - 1, sections)
    ring = (lax.rem(head + 2, heads_count), lax.rem(head + heads_count - 2, heads_count))

    barrier = pltpu.get_barrier_semaphore()
    for near in ring:
        pl.semaphore_signal(barrier, inc=1, device_id=(section, near), device_id_type=MESH)
    for other in range(2):
        for where in (after, prior):
            pl.semaphore_signal(
                barrier, inc=1, device_id=(where, 2 * y + other), device_id_type=MESH
            )
    pl.semaphore_wait(barrier, 6)

    res_copy = pltpu.make_async_remote_copy(
        src_ref=res_ref,
        dst_ref=res_land,
        send_sem=xsem.at[0],
        recv_sem=xsem.at[1],
        device_id=(after, head),
        device_id_type=MESH,
    )
    res_copy.start()

    def chunk_at(d, step):
        if d == 0:
            return lax.rem(y + 2 * ny - 1 - step, ny)
        return lax.rem(y + 1 + step, ny)

    def ring_copy(step, d, g):
        return pltpu.make_async_remote_copy(
            src_ref=buf.at[step, d, g],
            dst_ref=buf.at[step + 1, d, g],
            send_sem=ssem.at[step, d, g],
            recv_sem=rsem.at[step, d, g],
            device_id=(section, ring[d]),
            device_id_type=MESH,
        )

    def column_of(d, g):
        return d * half + (g % SPLIT) * wide

    def out_copy(d, g, target, source):
        t = g // SPLIT
        return pltpu.make_async_remote_copy(
            src_ref=buf.at[hops, d, g, pl.ds(target * own, own), :],
            dst_ref=land_ref.at[source, t, :, pl.ds(column_of(d, g), wide)],
            send_sem=zssem.at[d, g, target],
            recv_sem=zrsem.at[d, g, source],
            device_id=(after, 2 * y + target),
            device_id_type=MESH,
        )

    for g in range(groups):
        t = g // SPLIT
        for d in range(2):
            rows_at = pl.multiple_of(chunk_at(d, 0) * chunk, chunk)
            block = heads_ref[t, pl.ds(rows_at, chunk), :]
            column = column_of(d, g)
            buf[0, d, g] = jnp.dot(
                block, w_ref[:, column:column + wide], preferred_element_type=jnp.float32
            ).astype(jnp.bfloat16)
        if SKEW[g] == 0:
            for d in range(2):
                ring_copy(0, d, g).start()

    tile = min(512, 2 * half)

    def fill(i, carry):
        at = pl.multiple_of(i * tile, tile)
        for t in range(ticks):
            part[t, :, pl.ds(at, tile)] = jnp.dot(
                heads_ref[t], w_ref[:, pl.ds(at, tile)], preferred_element_type=jnp.float32
            ).astype(jnp.bfloat16)
        return carry

    lax.fori_loop(0, 2 * half // tile, fill, 0)

    def slot(now, carry):
        for g in range(groups):
            t = g // SPLIT
            step = now - SKEW[g]
            if SKEW[g] > 0:
                @pl.when(step == 0)
                def _(g=g):
                    for d in range(2):
                        ring_copy(0, d, g).start()

            @pl.when(jnp.logical_and(step >= 1, step <= hops))
            def _(g=g, t=t, step=step):
                for d in range(2):
                    ring_copy(step - 1, d, g).wait_recv()
                    rows_at = pl.multiple_of(chunk_at(d, step) * chunk, chunk)
                    column = column_of(d, g)
                    mine = part[t, pl.ds(rows_at, chunk), column:column + wide]
                    buf[step, d, g] = (
                        buf[step, d, g].astype(jnp.float32) + mine.astype(jnp.float32)
                    ).astype(jnp.bfloat16)

                    @pl.when(step < hops)
                    def _():
                        ring_copy(step, d, g).start()

                    @pl.when(step == hops)
                    def _():
                        for target in range(2):
                            out_copy(d, g, target, z).start()
        return carry

    lax.fori_loop(1, hops + 1 + max(SKEW), slot, 0)

    for d in range(2):
        for g in range(groups):
            for other in range(2):
                out_copy(d, g, other, other).wait_recv()
    for d in range(2):
        for g in range(groups):
            for other in range(2):
                out_copy(d, g, other, other).wait_send()

            def drain(step, carry, d=d, g=g):
                ring_copy(step, d, g).wait_send()
                return carry

            lax.fori_loop(0, hops, drain, 0)
    res_copy.wait()


def reduce_shift(heads, weight, residual, sections, heads_count):
    ticks, rows, width = heads.shape
    depth = weight.shape[1]
    ny = heads_count // 2
    hops = ny - 1
    groups = ticks * SPLIT
    chunk = rows // ny
    wide = depth // 2 // SPLIT
    any_space = pl.BlockSpec(memory_space=pl.ANY)
    vmem = pl.BlockSpec(memory_space=pltpu.VMEM)
    return pl.pallas_call(
        functools.partial(reduce_kernel, sections, heads_count),
        out_shape=(
            jax.ShapeDtypeStruct((2, ticks, chunk // 2, depth), jnp.bfloat16),
            jax.ShapeDtypeStruct(residual.shape, jnp.bfloat16),
        ),
        in_specs=[vmem, vmem, any_space],
        out_specs=(any_space, any_space),
        scratch_shapes=[
            pltpu.VMEM((ticks, rows, depth), jnp.bfloat16),
            pltpu.VMEM((hops + 1, 2, groups, chunk, wide), jnp.bfloat16),
            pltpu.SemaphoreType.DMA((hops, 2, groups)),
            pltpu.SemaphoreType.DMA((hops, 2, groups)),
            pltpu.SemaphoreType.DMA((2, groups, 2)),
            pltpu.SemaphoreType.DMA((2, groups, 2)),
            pltpu.SemaphoreType.DMA((2,)),
        ],
        compiler_params=pltpu.CompilerParams(collective_id=0, has_side_effects=True),
        name="reduce_shift",
    )(heads, weight, residual)


def on_device(residual, queries, new_kv, cache_kv, lengths, out_weight):
    sections = lax.axis_size("section")
    heads_count = lax.axis_size("head")
    heads = attend(queries, new_kv, cache_kv, lengths)
    land, moved = reduce_shift(heads, out_weight[0], residual, sections, heads_count)
    projected = land[0].astype(jnp.float32) + land[1].astype(jnp.float32)
    return (moved.astype(jnp.float32) + projected.transpose(1, 0, 2)).astype(jnp.bfloat16)


def solution(mesh):
    placed = (
        P(("section", "head"), None, None),
        P(None, "section", "head"),
        P(None, None, "section", None),
        P(None, "section", None),
        P(),
        P("section", "head", None),
    )
    return jax.shard_map(
        on_device,
        mesh=mesh,
        in_specs=placed,
        out_specs=P(("section", "head"), None, None),
        check_vma=False,
    )
```

```python
import functools
import math

import jax
import jax.numpy as jnp
from jax import lax
from jax.experimental import pallas as pl
from jax.experimental.pallas import tpu as pltpu
from jax.sharding import PartitionSpec as P

HD = 128
KBLK = 512
NEG = -1e30
SCALE = math.log2(math.e) / math.sqrt(HD)
SPLIT = 4
SKEW = (0, 0, 0, 0, 4, 4, 5, 5)
MESH = pl.DeviceIdType.MESH


def softmax_block(s, values, m_ref, l_ref, acc_ref, at):
    before = m_ref[at]
    m = jnp.maximum(before, jnp.max(s, axis=1, keepdims=True))
    p = jnp.exp2((s - m) * SCALE)
    factor = jnp.exp2((before - m) * SCALE)
    m_ref[at] = m
    l_ref[at] = l_ref[at] * factor + jnp.sum(p, axis=1, keepdims=True)
    acc_ref[at] = acc_ref[at] * factor + jnp.dot(
        p.astype(jnp.bfloat16), values, preferred_element_type=jnp.float32
    )


def scores_of(q, keys):
    return lax.dot_general(q, keys, (((1,), (1,)), ((), ())), preferred_element_type=jnp.float32)


def kv_column():
    return pl.multiple_of((lax.axis_index("head") // 2) * HD, HD)


def attend_kernel(
    len_ref, q_hbm, new_ref, cache_ref, o_ref, q_ref, fresh, cache, m_ref, l_ref, acc_ref, fsem, csem
):
    rows, width = q_ref.shape
    here = width // HD
    key_blocks = cache.shape[0]
    length = len_ref[lax.axis_index("section")]
    column = kv_column()
    used = (length + KBLK - 1) // KBLK

    def fresh_copy(i):
        return pltpu.make_async_copy(
            new_ref.at[0, i, :, pl.ds(column, HD)], fresh.at[i], fsem.at[i]
        )

    def cache_copy(b, i):
        return pltpu.make_async_copy(
            cache_ref.at[i, pl.ds(b * KBLK, KBLK), pl.ds(column, HD)],
            cache.at[b, i],
            csem.at[b, i],
        )

    q_copy = pltpu.make_async_copy(q_hbm.at[0], q_ref, fsem.at[2])
    q_copy.start()
    for i in range(2):
        fresh_copy(i).start()
    for b in range(key_blocks):
        @pl.when(b < used)
        def _(b=b):
            for i in range(2):
                cache_copy(b, i).start()
    q_copy.wait()
    for i in range(2):
        fresh_copy(i).wait()

    row_id = lax.broadcasted_iota(jnp.int32, (rows, rows), 0)
    col_id = lax.broadcasted_iota(jnp.int32, (rows, rows), 1)
    seen = col_id <= row_id
    for h in range(here):
        s = jnp.where(seen, scores_of(q_ref[:, h * HD:(h + 1) * HD], fresh[0]), NEG)
        m = jnp.max(s, axis=1, keepdims=True)
        p = jnp.exp2((s - m) * SCALE)
        m_ref[h] = m
        l_ref[h] = jnp.sum(p, axis=1, keepdims=True)
        acc_ref[h] = jnp.dot(
            p.astype(jnp.bfloat16), fresh[1], preferred_element_type=jnp.float32
        )

    def one_block(b, carry):
        for i in range(2):
            cache_copy(b, i).wait()
        seen = lax.broadcasted_iota(jnp.int32, (1, KBLK), 1) + b * KBLK < length
        for h in range(here):
            s = scores_of(q_ref[:, h * HD:(h + 1) * HD], cache[b, 0])
            softmax_block(jnp.where(seen, s, NEG), cache[b, 1], m_ref, l_ref, acc_ref, h)
        return carry

    lax.fori_loop(0, used, one_block, 0)
    for h in range(here):
        o_ref[:, h * HD:(h + 1) * HD] = (acc_ref[h] / l_ref[h]).astype(jnp.bfloat16)


def attend(queries, new_kv, cache_kv, lengths):
    ticks, rows, width = queries.shape
    here = width // HD
    blocks = cache_kv.shape[1] // KBLK
    any_space = pl.BlockSpec(memory_space=pl.ANY)
    return pl.pallas_call(
        attend_kernel,
        out_shape=jax.ShapeDtypeStruct((rows, width), jnp.bfloat16),
        in_specs=[pl.BlockSpec(memory_space=pltpu.SMEM), any_space, any_space, any_space],
        out_specs=pl.BlockSpec(memory_space=pltpu.VMEM),
        scratch_shapes=[
            pltpu.VMEM((rows, width), jnp.bfloat16),
            pltpu.VMEM((2, rows, HD), jnp.bfloat16),
            pltpu.VMEM((blocks, 2, KBLK, HD), jnp.bfloat16),
            pltpu.VMEM((here, rows, 1), jnp.float32),
            pltpu.VMEM((here, rows, 1), jnp.float32),
            pltpu.VMEM((here, rows, HD), jnp.float32),
            pltpu.SemaphoreType.DMA((3,)),
            pltpu.SemaphoreType.DMA((blocks, 2)),
        ],
        name="attend",
    )(lengths, queries, new_kv, cache_kv)


def reduce_kernel(
    sections,
    heads_count,
    len_ref,
    heads_hbm,
    w_hbm,
    q_hbm,
    new_ref,
    cache_ref,
    res_ref,
    proj_ref,
    res_land,
    heads_ref,
    w_ref,
    q_ref,
    kv,
    m_ref,
    l_ref,
    acc_ref,
    part,
    buf,
    land,
    isem,
    wsem,
    kvsem,
    ssem,
    rsem,
    zssem,
    zrsem,
    xsem,
):
    ny = heads_count // 2
    hops = ny - 1
    groups = buf.shape[2]
    ticks, rows, width = heads_ref.shape
    here = width // HD
    chunk = buf.shape[3]
    wide = buf.shape[4]
    own = chunk // 2
    half = w_ref.shape[1] // 2
    key_blocks = kv.shape[0]
    quarter = rows // 2
    section = lax.axis_index("section")
    head = lax.axis_index("head")
    y = head // 2
    z = head % 2
    after = lax.rem(section + 1, sections)
    prior = lax.rem(section + sections - 1, sections)
    ring = (lax.rem(head + 2, heads_count), lax.rem(head + heads_count - 2, heads_count))
    column = kv_column()

    def column_of(d, g):
        return d * half + (g % SPLIT) * wide

    heads_copy = pltpu.make_async_copy(heads_hbm, heads_ref.at[0], isem.at[0])
    q_copy = pltpu.make_async_copy(q_hbm.at[1], q_ref, isem.at[1])

    def w_copy(d, g):
        at = column_of(d, g)
        return pltpu.make_async_copy(
            w_hbm.at[:, at:at + wide], w_ref.at[:, at:at + wide], wsem.at[d, g]
        )

    def fresh_copy(t, i):
        return pltpu.make_async_copy(
            new_ref.at[t, i, :, pl.ds(column, HD)],
            kv.at[0, i, pl.ds(t * rows, rows), :],
            kvsem.at[0, t, i],
        )

    def cache_copy(b, i):
        return pltpu.make_async_copy(
            cache_ref.at[i, pl.ds((b - 1) * KBLK, KBLK), pl.ds(column, HD)],
            kv.at[b, i],
            kvsem.at[b, 0, i],
        )

    heads_copy.start()
    for g in range(SPLIT):
        for d in range(2):
            w_copy(d, g).start()
    q_copy.start()
    for i in range(2):
        for t in range(ticks):
            fresh_copy(t, i).start()
        for b in range(1, key_blocks):
            cache_copy(b, i).start()

    barrier = pltpu.get_barrier_semaphore()
    for near in ring:
        pl.semaphore_signal(barrier, inc=1, device_id=(section, near), device_id_type=MESH)
    for other in range(2):
        for where in (after, prior):
            pl.semaphore_signal(
                barrier, inc=1, device_id=(where, 2 * y + other), device_id_type=MESH
            )

    def chunk_at(d, step):
        if d == 0:
            return lax.rem(y + 2 * ny - 1 - step, ny)
        return lax.rem(y + 1 + step, ny)

    def chunk_rows(d, step):
        return pl.ds(pl.multiple_of(chunk_at(d, step) * chunk, chunk), chunk)

    def ring_copy(step, d, g):
        return pltpu.make_async_remote_copy(
            src_ref=buf.at[step, d, g],
            dst_ref=buf.at[step + 1, d, g],
            send_sem=ssem.at[step, d, g],
            recv_sem=rsem.at[step, d, g],
            device_id=(section, ring[d]),
            device_id_type=MESH,
        )

    def out_copy(d, g, target, source):
        return pltpu.make_async_remote_copy(
            src_ref=buf.at[hops, d, g, pl.ds(target * own, own), :],
            dst_ref=land.at[source, d, g],
            send_sem=zssem.at[d, g, target],
            recv_sem=zrsem.at[d, g, source],
            device_id=(after, 2 * y + target),
            device_id_type=MESH,
        )

    def first_block(d, g):
        at = column_of(d, g)
        w_copy(d, g).wait()
        buf[0, d, g] = jnp.dot(
            heads_ref[0, chunk_rows(d, 0), :],
            w_ref[:, at:at + wide],
            preferred_element_type=jnp.float32,
        ).astype(jnp.bfloat16)

    heads_copy.wait()
    for d in range(2):
        first_block(d, 0)
    pl.semaphore_wait(barrier, 6)
    for d in range(2):
        ring_copy(0, d, 0).start()
    for g in range(1, SPLIT):
        for d in range(2):
            first_block(d, g)
            ring_copy(0, d, g).start()
    res_copy = pltpu.make_async_remote_copy(
        src_ref=res_ref,
        dst_ref=res_land,
        send_sem=xsem.at[0],
        recv_sem=xsem.at[1],
        device_id=(after, head),
        device_id_type=MESH,
    )
    res_copy.start()

    tile = min(512, 2 * half)

    def fill(t):
        def one(i, carry):
            at = pl.multiple_of(i * tile, tile)
            part[t, :, pl.ds(at, tile)] = jnp.dot(
                heads_ref[t], w_ref[:, pl.ds(at, tile)], preferred_element_type=jnp.float32
            ).astype(jnp.bfloat16)
            return carry

        lax.fori_loop(0, 2 * half // tile, one, 0)

    fill(0)
    m_ref[...] = jnp.full_like(m_ref, NEG)
    l_ref[...] = jnp.zeros_like(l_ref)
    acc_ref[...] = jnp.zeros_like(acc_ref)
    length = len_ref[section]
    q_copy.wait()
    for i in range(2):
        for t in range(ticks):
            fresh_copy(t, i).wait()
        for b in range(1, key_blocks):
            cache_copy(b, i).wait()

    def piece(b, at):
        h, r = at // 2, at % 2
        row_id = lax.broadcasted_iota(jnp.int32, (quarter, 1), 0) + r * quarter
        limit = jnp.where(b == 0, row_id + rows + 1, length - (b - 1) * KBLK)
        seen = lax.broadcasted_iota(jnp.int32, (quarter, KBLK), 1) < limit
        s = scores_of(q_ref[r * quarter:(r + 1) * quarter, h * HD:(h + 1) * HD], kv[b, 0])
        softmax_block(jnp.where(seen, s, NEG), kv[b, 1], m_ref, l_ref, acc_ref, at)

    def second_start(d, g):
        at = column_of(d, g)
        buf[0, d, g] = part[1, chunk_rows(d, 0), at:at + wide]
        ring_copy(0, d, g).start()

    def slot(now, carry):
        for g in range(groups):
            t = g // SPLIT
            step = now - SKEW[g]
            if SKEW[g] > key_blocks:
                @pl.when(step == 0)
                def _(g=g):
                    for d in range(2):
                        second_start(d, g)

            @pl.when(jnp.logical_and(step >= 1, step <= hops))
            def _(g=g, t=t, step=step):
                for d in range(2):
                    ring_copy(step - 1, d, g).wait_recv()
                    at = column_of(d, g)
                    mine = part[t, chunk_rows(d, step), at:at + wide]
                    buf[step, d, g] = (
                        buf[step, d, g].astype(jnp.float32) + mine.astype(jnp.float32)
                    ).astype(jnp.bfloat16)

                    @pl.when(step < hops)
                    def _():
                        ring_copy(step, d, g).start()

                    @pl.when(step == hops)
                    def _():
                        for target in range(2):
                            out_copy(d, g, target, z).start()

            if g < 2 * here:
                @pl.when(now <= key_blocks)
                def _(g=g):
                    piece(now - 1, g)

        @pl.when(now == key_blocks)
        def _():
            for at in range(2 * here):
                h, r = at // 2, at % 2
                heads_ref[1, r * quarter:(r + 1) * quarter, h * HD:(h + 1) * HD] = (
                    acc_ref[at] / l_ref[at]
                ).astype(jnp.bfloat16)
            fill(1)
            for g in range(SPLIT, groups):
                if SKEW[g] == key_blocks:
                    for d in range(2):
                        second_start(d, g)

        return carry

    lax.fori_loop(1, hops + 1 + max(SKEW), slot, 0)

    for g in range(groups):
        for d in range(2):
            for other in range(2):
                out_copy(d, g, other, other).wait_recv()
            at = column_of(d, g)
            proj_ref[g // SPLIT, :, at:at + wide] = (
                land[0, d, g].astype(jnp.float32) + land[1, d, g].astype(jnp.float32)
            ).astype(proj_ref.dtype)
    for d in range(2):
        for g in range(groups):
            for other in range(2):
                out_copy(d, g, other, other).wait_send()

            def drain(step, carry, d=d, g=g):
                ring_copy(step, d, g).wait_send()
                return carry

            lax.fori_loop(0, hops, drain, 0)
    res_copy.wait()


def reduce_shift(lengths, heads, weight, queries, new_kv, cache_kv, residual, sections, heads_count):
    ticks, rows, width = queries.shape
    here = width // HD
    depth = weight.shape[1]
    ny = heads_count // 2
    hops = ny - 1
    groups = ticks * SPLIT
    chunk = rows // ny
    wide = depth // 2 // SPLIT
    blocks = cache_kv.shape[1] // KBLK + 1
    any_space = pl.BlockSpec(memory_space=pl.ANY)
    return pl.pallas_call(
        functools.partial(reduce_kernel, sections, heads_count),
        out_shape=(
            jax.ShapeDtypeStruct((ticks, chunk // 2, depth), jnp.bfloat16),
            jax.ShapeDtypeStruct(residual.shape, jnp.bfloat16),
        ),
        in_specs=[pl.BlockSpec(memory_space=pltpu.SMEM)] + [any_space] * 6,
        out_specs=(pl.BlockSpec(memory_space=pltpu.VMEM), any_space),
        scratch_shapes=[
            pltpu.VMEM((ticks, rows, width), jnp.bfloat16),
            pltpu.VMEM(weight.shape, jnp.bfloat16),
            pltpu.VMEM((rows, width), jnp.bfloat16),
            pltpu.VMEM((blocks, 2, KBLK, HD), jnp.bfloat16),
            pltpu.VMEM((2 * here, rows // 2, 1), jnp.float32),
            pltpu.VMEM((2 * here, rows // 2, 1), jnp.float32),
            pltpu.VMEM((2 * here, rows // 2, HD), jnp.float32),
            pltpu.VMEM((ticks, rows, depth), jnp.bfloat16),
            pltpu.VMEM((hops + 1, 2, groups, chunk, wide), jnp.bfloat16),
            pltpu.VMEM((2, 2, groups, chunk // 2, wide), jnp.bfloat16),
            pltpu.SemaphoreType.DMA((2,)),
            pltpu.SemaphoreType.DMA((2, SPLIT)),
            pltpu.SemaphoreType.DMA((blocks, 2, 2)),
            pltpu.SemaphoreType.DMA((hops, 2, groups)),
            pltpu.SemaphoreType.DMA((hops, 2, groups)),
            pltpu.SemaphoreType.DMA((2, groups, 2)),
            pltpu.SemaphoreType.DMA((2, groups, 2)),
            pltpu.SemaphoreType.DMA((2,)),
        ],
        compiler_params=pltpu.CompilerParams(collective_id=0, has_side_effects=True),
        name="reduce_shift",
    )(lengths, heads, weight, queries, new_kv, cache_kv, residual)


def on_device(residual, queries, new_kv, cache_kv, lengths, out_weight):
    sections = lax.axis_size("section")
    heads_count = lax.axis_size("head")
    heads = attend(queries, new_kv, cache_kv, lengths)
    projected, moved = reduce_shift(
        lengths, heads, out_weight[0], queries, new_kv, cache_kv, residual, sections, heads_count
    )
    projected = projected.astype(jnp.float32).transpose(1, 0, 2)
    return (moved.astype(jnp.float32) + projected).astype(jnp.bfloat16)


def solution(mesh):
    placed = (
        P(("section", "head"), None, None),
        P(None, "section", "head"),
        P(None, None, "section", None),
        P(None, "section", None),
        P(),
        P("section", "head", None),
    )
    return jax.shard_map(
        on_device,
        mesh=mesh,
        in_specs=placed,
        out_specs=P(("section", "head"), None, None),
        check_vma=False,
    )
```

```python
import functools
import math

import jax
import jax.numpy as jnp
from jax import lax
from jax.experimental import pallas as pl
from jax.experimental.pallas import tpu as pltpu
from jax.sharding import PartitionSpec as P

HD = 128
NEG = -1e30
SCALE = math.log2(math.e) / math.sqrt(HD)
SPLIT = 4
SKEW = (0, 0, 0, 0, 4, 4, 5, 5)
MESH = pl.DeviceIdType.MESH


def reduce_kernel(
    sections,
    heads_count,
    len_ref,
    q_hbm,
    new_ref,
    cache_ref,
    w_hbm,
    res_ref,
    out_ref,
    q_ref,
    kv,
    w_ref,
    mixed,
    part,
    buf,
    land,
    moved,
    summed,
    isem,
    wsem,
    ssem,
    rsem,
    zssem,
    zrsem,
    xsem,
):
    ny = heads_count // 2
    hops = ny - 1
    pairs = ny // 2
    groups = buf.shape[2]
    ticks, rows, width = q_ref.shape
    here = width // HD
    chunk = buf.shape[3]
    wide = buf.shape[4]
    own = chunk // 2
    half = w_ref.shape[1] // 2
    cached = cache_ref.shape[1]
    section = lax.axis_index("section")
    head = lax.axis_index("head")
    y = head // 2
    z = head % 2
    after = lax.rem(section + 1, sections)
    prior = lax.rem(section + sections - 1, sections)
    ring = (lax.rem(head + 2, heads_count), lax.rem(head + heads_count - 2, heads_count))
    column = pl.multiple_of((head // 2) * HD, HD)

    def column_of(d, g):
        return d * half + (g % SPLIT) * wide

    def w_copy(d, g):
        at = column_of(d, g)
        return pltpu.make_async_copy(
            w_hbm.at[:, at:at + wide], w_ref.at[:, at:at + wide], wsem.at[d, g]
        )

    def fresh_copy(t, i):
        at = t * (rows + cached)
        return pltpu.make_async_copy(
            new_ref.at[t, i, :, pl.ds(column, HD)],
            kv.at[i, at:at + rows, :],
            isem.at[1 + t, i],
        )

    def cache_copy(i):
        return pltpu.make_async_copy(
            cache_ref.at[i, :, pl.ds(column, HD)],
            kv.at[i, rows:rows + cached, :],
            isem.at[3, i],
        )

    q_copy = pltpu.make_async_copy(q_hbm, q_ref, isem.at[0, 0])
    q_copy.start()
    for i in range(2):
        fresh_copy(0, i).start()
        cache_copy(i).start()
    for g in range(SPLIT):
        for d in range(2):
            w_copy(d, g).start()
    for i in range(2):
        fresh_copy(1, i).start()

    barrier = pltpu.get_barrier_semaphore()
    for near in ring:
        pl.semaphore_signal(barrier, inc=1, device_id=(section, near), device_id_type=MESH)
    for other in range(2):
        for where in (after, prior):
            pl.semaphore_signal(
                barrier, inc=1, device_id=(where, 2 * y + other), device_id_type=MESH
            )

    def chunk_at(d, step):
        if d == 0:
            return lax.rem(y + 2 * ny - 1 - step, ny)
        return lax.rem(y + 1 + step, ny)

    def rows_of(c):
        return pl.ds(pl.multiple_of(c * chunk, chunk), chunk)

    def ring_copy(step, d, g):
        return pltpu.make_async_remote_copy(
            src_ref=buf.at[step, d, g],
            dst_ref=buf.at[step + 1, d, g],
            send_sem=ssem.at[step, d, g],
            recv_sem=rsem.at[step, d, g],
            device_id=(section, ring[d]),
            device_id_type=MESH,
        )

    def out_copy(d, g, target, source):
        return pltpu.make_async_remote_copy(
            src_ref=buf.at[hops, d, g, pl.ds(target * own, own), :],
            dst_ref=land.at[source, d, g],
            send_sem=zssem.at[d, g, target],
            recv_sem=zrsem.at[d, g, source],
            device_id=(after, 2 * y + target),
            device_id_type=MESH,
        )

    length = len_ref[section]

    def pair_of(p):
        return chunk_at(0, p), jnp.where(p == pairs - 1, y, chunk_at(1, p))

    def attend(t, p):
        pair = pair_of(p)
        q = jnp.concatenate(
            [q_ref[t, rows_of(c), h * HD:(h + 1) * HD] for h in range(here) for c in pair], axis=0
        )
        base = lax.broadcasted_iota(jnp.int32, (chunk, 1), 0)
        place = jnp.concatenate([base + c * chunk for h in range(here) for c in pair], axis=0)

        def scores(first, count):
            return lax.dot_general(
                q,
                kv[0, first:first + count, :],
                (((1,), (1,)), ((), ())),
                preferred_element_type=jnp.float32,
            )

        local = lax.broadcasted_iota(jnp.int32, (chunk * 2 * here, rows), 1)
        held = lax.broadcasted_iota(jnp.int32, (1, cached), 1)
        blocks = []
        first_block = scores(0, rows)
        blocks.append(jnp.where(local <= place, first_block, NEG) if t == 0 else first_block)
        blocks.append(jnp.where(held < length, scores(rows, cached), NEG))
        if t == 1:
            blocks.append(jnp.where(local <= place, scores(rows + cached, rows), NEG))
        s = jnp.concatenate(blocks, axis=1)
        m = jnp.max(s, axis=1, keepdims=True)
        w = jnp.exp2((s - m) * SCALE)
        total = jnp.sum(w, axis=1, keepdims=True)
        o = jnp.dot(
            w.astype(jnp.bfloat16), kv[1, 0:s.shape[1], :], preferred_element_type=jnp.float32
        )
        o = (o / total).astype(jnp.bfloat16)
        for h in range(here):
            mixed[:, h * HD:(h + 1) * HD] = o[2 * chunk * h:2 * chunk * (h + 1)]

    def project(t, p, d, g):
        pair = pair_of(p)
        at = column_of(d, g)
        block = jnp.dot(
            mixed[...], w_ref[:, at:at + wide], preferred_element_type=jnp.float32
        ).astype(jnp.bfloat16)
        for i in range(2):
            part[t, rows_of(pair[i]), at:at + wide] = block[i * chunk:(i + 1) * chunk]
        return block

    q_copy.wait()
    for i in range(2):
        fresh_copy(0, i).wait()
        cache_copy(i).wait()
    attend(0, 0)
    for g in range(SPLIT):
        for d in range(2):
            w_copy(d, g).wait()
            buf[0, d, g] = project(0, 0, d, g)[d * chunk:(d + 1) * chunk]
        if g == 0:
            pl.semaphore_wait(barrier, 6)
        for d in range(2):
            ring_copy(0, d, g).start()
    res_copy = pltpu.make_async_remote_copy(
        src_ref=res_ref,
        dst_ref=moved,
        send_sem=xsem.at[0],
        recv_sem=xsem.at[1],
        device_id=(after, head),
        device_id_type=MESH,
    )
    res_copy.start()
    for i in range(2):
        fresh_copy(1, i).wait()

    def attend_next(k):
        for t in range(ticks):
            @pl.when(jnp.logical_and(k >= t * pairs, k < (t + 1) * pairs))
            def _(t=t):
                attend(t, k - t * pairs)

    def project_next(k, d):
        for t in range(ticks):
            @pl.when(jnp.logical_and(k >= t * pairs, k < (t + 1) * pairs))
            def _(t=t):
                for g in range(SPLIT):
                    project(t, k - t * pairs, d, g)

    attend_next(1)
    for d in range(2):
        project_next(1, d)

    def slot(now, carry):
        for g in range(SPLIT, groups):
            @pl.when(now == SKEW[g])
            def _(g=g):
                for d in range(2):
                    at = column_of(d, g)
                    buf[0, d, g] = part[1, rows_of(chunk_at(d, 0)), at:at + wide]
                    ring_copy(0, d, g).start()

        for g in range(groups):
            t = g // SPLIT
            step = now - SKEW[g]

            @pl.when(jnp.logical_and(step >= 1, step <= hops))
            def _(g=g, t=t, step=step):
                for d in range(2):
                    ring_copy(step - 1, d, g).wait_recv()
                    at = column_of(d, g)
                    mine = part[t, rows_of(chunk_at(d, step)), at:at + wide]
                    buf[step, d, g] = (
                        buf[step, d, g].astype(jnp.float32) + mine.astype(jnp.float32)
                    ).astype(jnp.bfloat16)

                    @pl.when(step < hops)
                    def _():
                        ring_copy(step, d, g).start()

                    @pl.when(step == hops)
                    def _():
                        for target in range(2):
                            out_copy(d, g, target, z).start()

            if g == 1:
                attend_next(now + 1)
            if g == 2 or g == 3:
                project_next(now + 1, g - 2)

        return carry

    lax.fori_loop(1, hops + 1 + max(SKEW), slot, 0)

    res_copy.wait_recv()
    for g in range(groups):
        for d in range(2):
            for other in range(2):
                out_copy(d, g, other, other).wait_recv()
            at = column_of(d, g)
            summed[:, g // SPLIT, at:at + wide] = land[0, d, g].astype(jnp.float32) + land[
                1, d, g
            ].astype(jnp.float32)
            if g >= groups - SPLIT:
                out_ref[:, :, at:at + wide] = (
                    summed[:, :, at:at + wide] + moved[:, :, at:at + wide].astype(jnp.float32)
                ).astype(jnp.bfloat16)
    for d in range(2):
        for g in range(groups):
            for other in range(2):
                out_copy(d, g, other, other).wait_send()

            def drain(step, carry, d=d, g=g):
                ring_copy(step, d, g).wait_send()
                return carry

            lax.fori_loop(0, hops, drain, 0)
    res_copy.wait_send()


def on_device(residual, queries, new_kv, cache_kv, lengths, out_weight):
    sections = lax.axis_size("section")
    heads_count = lax.axis_size("head")
    weight = out_weight[0]
    ticks, rows, width = queries.shape
    depth = weight.shape[1]
    ny = heads_count // 2
    hops = ny - 1
    groups = ticks * SPLIT
    chunk = rows // ny
    wide = depth // 2 // SPLIT
    keys = cache_kv.shape[1] + ticks * rows
    any_space = pl.BlockSpec(memory_space=pl.ANY)
    return pl.pallas_call(
        functools.partial(reduce_kernel, sections, heads_count),
        out_shape=jax.ShapeDtypeStruct(residual.shape, jnp.bfloat16),
        in_specs=[pl.BlockSpec(memory_space=pltpu.SMEM)] + [any_space] * 5,
        out_specs=pl.BlockSpec(memory_space=pltpu.VMEM),
        scratch_shapes=[
            pltpu.VMEM((ticks, rows, width), jnp.bfloat16),
            pltpu.VMEM((2, keys, HD), jnp.bfloat16),
            pltpu.VMEM(weight.shape, jnp.bfloat16),
            pltpu.VMEM((2 * chunk, width), jnp.bfloat16),
            pltpu.VMEM((ticks, rows, depth), jnp.bfloat16),
            pltpu.VMEM((hops + 1, 2, groups, chunk, wide), jnp.bfloat16),
            pltpu.VMEM((2, 2, groups, chunk // 2, wide), jnp.bfloat16),
            pltpu.VMEM(residual.shape, jnp.bfloat16),
            pltpu.VMEM(residual.shape, jnp.float32),
            pltpu.SemaphoreType.DMA((4, 2)),
            pltpu.SemaphoreType.DMA((2, SPLIT)),
            pltpu.SemaphoreType.DMA((hops, 2, groups)),
            pltpu.SemaphoreType.DMA((hops, 2, groups)),
            pltpu.SemaphoreType.DMA((2, groups, 2)),
            pltpu.SemaphoreType.DMA((2, groups, 2)),
            pltpu.SemaphoreType.DMA((2,)),
        ],
        compiler_params=pltpu.CompilerParams(collective_id=0, has_side_effects=True),
        name="attend_reduce_shift",
    )(lengths, queries, new_kv, cache_kv, weight, residual)


def solution(mesh):
    placed = (
        P(("section", "head"), None, None),
        P(None, "section", "head"),
        P(None, None, "section", None),
        P(None, "section", None),
        P(),
        P("section", "head", None),
    )
    return jax.shard_map(
        on_device,
        mesh=mesh,
        in_specs=placed,
        out_specs=P(("section", "head"), None, None),
        check_vma=False,
    )
```

```python
import functools
import math

import jax
import jax.numpy as jnp
from jax import lax
from jax.experimental import pallas as pl
from jax.experimental.pallas import tpu as pltpu
from jax.sharding import PartitionSpec as P

HD = 128
NEG = -1e30
SCALE = math.log2(math.e) / math.sqrt(HD)
SPLIT = 4
LAG = 3
SKEW = (0,) * SPLIT + (LAG,) * SPLIT
MESH = pl.DeviceIdType.MESH


def reduce_kernel(
    sections,
    heads_count,
    len_ref,
    q_hbm,
    new_ref,
    cache_ref,
    w_hbm,
    res_ref,
    out_ref,
    q_ref,
    kv,
    w_ref,
    mixed,
    part,
    buf,
    land,
    moved,
    summed,
    isem,
    wsem,
    ssem,
    rsem,
    zssem,
    zrsem,
    xsem,
):
    ny = heads_count // 2
    hops = ny - 1
    pairs = ny // 2
    groups = buf.shape[2]
    ticks, rows, width = q_ref.shape
    here = width // HD
    chunk = buf.shape[3]
    wide = buf.shape[4]
    own = chunk // 2
    half = w_ref.shape[1] // 2
    cached = cache_ref.shape[1]
    section = lax.axis_index("section")
    head = lax.axis_index("head")
    y = head // 2
    z = head % 2
    after = lax.rem(section + 1, sections)
    prior = lax.rem(section + sections - 1, sections)
    ring = (lax.rem(head + 2, heads_count), lax.rem(head + heads_count - 2, heads_count))
    column = pl.multiple_of((head // 2) * HD, HD)

    def column_of(d, g):
        return d * half + (g % SPLIT) * wide

    def w_copy(d, g):
        at = column_of(d, g)
        return pltpu.make_async_copy(
            w_hbm.at[:, at:at + wide], w_ref.at[:, at:at + wide], wsem.at[d, g]
        )

    def fresh_copy(t, i):
        at = t * (rows + cached)
        return pltpu.make_async_copy(
            new_ref.at[t, i, :, pl.ds(column, HD)],
            kv.at[i, at:at + rows, :],
            isem.at[1 + t, i],
        )

    def cache_copy(i):
        return pltpu.make_async_copy(
            cache_ref.at[i, :, pl.ds(column, HD)],
            kv.at[i, rows:rows + cached, :],
            isem.at[3, i],
        )

    q_copy = pltpu.make_async_copy(q_hbm, q_ref, isem.at[0, 0])
    q_copy.start()
    for i in range(2):
        fresh_copy(0, i).start()
        cache_copy(i).start()
    for g in range(SPLIT):
        for d in range(2):
            w_copy(d, g).start()
    for i in range(2):
        fresh_copy(1, i).start()

    barrier = pltpu.get_barrier_semaphore()
    for near in ring:
        pl.semaphore_signal(barrier, inc=1, device_id=(section, near), device_id_type=MESH)
    for other in range(2):
        for where in (after, prior):
            pl.semaphore_signal(
                barrier, inc=1, device_id=(where, 2 * y + other), device_id_type=MESH
            )

    def chunk_at(d, step):
        if d == 0:
            return lax.rem(y + 2 * ny - 1 - step, ny)
        return lax.rem(y + 1 + step, ny)

    def rows_of(c):
        return pl.ds(pl.multiple_of(c * chunk, chunk), chunk)

    def ring_copy(step, d, g):
        return pltpu.make_async_remote_copy(
            src_ref=buf.at[step, d, g],
            dst_ref=buf.at[step + 1, d, g],
            send_sem=ssem.at[step, d, g],
            recv_sem=rsem.at[step, d, g],
            device_id=(section, ring[d]),
            device_id_type=MESH,
        )

    def out_copy(d, g, target, source):
        return pltpu.make_async_remote_copy(
            src_ref=buf.at[hops, d, g, pl.ds(target * own, own), :],
            dst_ref=land.at[source, d, g],
            send_sem=zssem.at[d, g, target],
            recv_sem=zrsem.at[d, g, source],
            device_id=(after, 2 * y + target),
            device_id_type=MESH,
        )

    length = len_ref[section]

    def pair_of(p):
        return chunk_at(0, p), jnp.where(p == pairs - 1, y, chunk_at(1, p))

    def attend(t, p, before_values=None):
        pair = pair_of(p)
        q = jnp.concatenate(
            [q_ref[t, rows_of(c), h * HD:(h + 1) * HD] for h in range(here) for c in pair], axis=0
        )
        base = lax.broadcasted_iota(jnp.int32, (chunk, 1), 0)
        place = jnp.concatenate([base + c * chunk for h in range(here) for c in pair], axis=0)

        def scores(first, count):
            return lax.dot_general(
                q,
                kv[0, first:first + count, :],
                (((1,), (1,)), ((), ())),
                preferred_element_type=jnp.float32,
            )

        local = lax.broadcasted_iota(jnp.int32, (chunk * 2 * here, rows), 1)
        held = lax.broadcasted_iota(jnp.int32, (1, cached), 1)
        blocks = []
        first_block = scores(0, rows)
        blocks.append(jnp.where(local <= place, first_block, NEG) if t == 0 else first_block)
        blocks.append(jnp.where(held < length, scores(rows, cached), NEG))
        if t == 1:
            blocks.append(jnp.where(local <= place, scores(rows + cached, rows), NEG))
        s = jnp.concatenate(blocks, axis=1)
        m = jnp.max(s, axis=1, keepdims=True)
        w = jnp.exp2((s - m) * SCALE)
        total = jnp.sum(w, axis=1, keepdims=True)
        if before_values is not None:
            before_values()
        o = jnp.dot(
            w.astype(jnp.bfloat16), kv[1, 0:s.shape[1], :], preferred_element_type=jnp.float32
        )
        o = (o / total).astype(jnp.bfloat16)
        for h in range(here):
            mixed[t, :, h * HD:(h + 1) * HD] = o[2 * chunk * h:2 * chunk * (h + 1)]

    def project(t, p, d, g):
        pair = pair_of(p)
        at = column_of(d, g)
        block = jnp.dot(
            mixed[t], w_ref[:, at:at + wide], preferred_element_type=jnp.float32
        ).astype(jnp.bfloat16)
        for i in range(2):
            part[t, rows_of(pair[i]), at:at + wide] = block[i * chunk:(i + 1) * chunk]
        return block

    def values_here():
        fresh_copy(0, 1).wait()
        cache_copy(1).wait()

    q_copy.wait()
    fresh_copy(0, 0).wait()
    cache_copy(0).wait()
    attend(0, 0, values_here)
    for g in range(SPLIT):
        for d in range(2):
            w_copy(d, g).wait()
            buf[0, d, g] = project(0, 0, d, g)[d * chunk:(d + 1) * chunk]
        if g == 0:
            pl.semaphore_wait(barrier, 6)
        for d in range(2):
            ring_copy(0, d, g).start()
    res_copy = pltpu.make_async_remote_copy(
        src_ref=res_ref,
        dst_ref=moved,
        send_sem=xsem.at[0],
        recv_sem=xsem.at[1],
        device_id=(after, head),
        device_id_type=MESH,
    )
    res_copy.start()
    for i in range(2):
        fresh_copy(1, i).wait()

    def attend_next(k):
        for t in range(ticks):
            @pl.when(jnp.logical_and(k >= t * LAG, k < t * LAG + pairs))
            def _(t=t):
                attend(t, k - t * LAG)

    def project_next(k, d):
        for t in range(ticks):
            @pl.when(jnp.logical_and(k >= t * LAG, k < t * LAG + pairs))
            def _(t=t):
                for g in range(SPLIT):
                    project(t, k - t * LAG, d, g)

    attend_next(1)
    for d in range(2):
        project_next(1, d)

    def slot(now, carry):
        for g in range(SPLIT, groups):
            @pl.when(now == SKEW[g])
            def _(g=g):
                for d in range(2):
                    at = column_of(d, g)
                    buf[0, d, g] = part[1, rows_of(chunk_at(d, 0)), at:at + wide]
                    ring_copy(0, d, g).start()

        for g in range(groups):
            t = g // SPLIT
            step = now - SKEW[g]

            @pl.when(jnp.logical_and(step >= 1, step <= hops))
            def _(g=g, t=t, step=step):
                for d in range(2):
                    ring_copy(step - 1, d, g).wait_recv()
                    at = column_of(d, g)
                    mine = part[t, rows_of(chunk_at(d, step)), at:at + wide]
                    buf[step, d, g] = (
                        buf[step, d, g].astype(jnp.float32) + mine.astype(jnp.float32)
                    ).astype(jnp.bfloat16)

                    @pl.when(step < hops)
                    def _():
                        ring_copy(step, d, g).start()

                    @pl.when(step == hops)
                    def _():
                        for target in range(2):
                            out_copy(d, g, target, z).start()

            if g == SPLIT // 4:
                attend_next(now + 1)
            if g == SPLIT // 2:
                project_next(now + 1, 0)
            if g == SPLIT - 1:
                project_next(now + 1, 1)

        return carry

    lax.fori_loop(1, hops + 1 + max(SKEW), slot, 0)

    res_copy.wait_recv()
    for g in range(groups):
        for d in range(2):
            for other in range(2):
                out_copy(d, g, other, other).wait_recv()
            at = column_of(d, g)
            summed[:, g // SPLIT, at:at + wide] = land[0, d, g].astype(jnp.float32) + land[
                1, d, g
            ].astype(jnp.float32)
            if g >= groups - SPLIT:
                out_ref[:, :, at:at + wide] = (
                    summed[:, :, at:at + wide] + moved[:, :, at:at + wide].astype(jnp.float32)
                ).astype(jnp.bfloat16)
    for d in range(2):
        for g in range(groups):
            for other in range(2):
                out_copy(d, g, other, other).wait_send()

            def drain(step, carry, d=d, g=g):
                ring_copy(step, d, g).wait_send()
                return carry

            lax.fori_loop(0, hops, drain, 0)
    res_copy.wait_send()


def hand_over_kernel(in_ref, out_ref, sem):
    copy = pltpu.make_async_copy(in_ref, out_ref, sem)
    copy.start()
    copy.wait()


def on_device(residual, queries, new_kv, cache_kv, lengths, out_weight):
    sections = lax.axis_size("section")
    heads_count = lax.axis_size("head")
    weight = out_weight[0]
    ticks, rows, width = queries.shape
    depth = weight.shape[1]
    ny = heads_count // 2
    hops = ny - 1
    groups = ticks * SPLIT
    chunk = rows // ny
    wide = depth // 2 // SPLIT
    keys = cache_kv.shape[1] + ticks * rows
    any_space = pl.BlockSpec(memory_space=pl.ANY)
    result = pl.pallas_call(
        functools.partial(reduce_kernel, sections, heads_count),
        out_shape=jax.ShapeDtypeStruct(residual.shape, jnp.bfloat16),
        in_specs=[pl.BlockSpec(memory_space=pltpu.SMEM)]
        + [pl.BlockSpec(memory_space=pltpu.HBM)] * 5,
        out_specs=pl.BlockSpec(memory_space=pltpu.VMEM),
        scratch_shapes=[
            pltpu.VMEM((ticks, rows, width), jnp.bfloat16),
            pltpu.VMEM((2, keys, HD), jnp.bfloat16),
            pltpu.VMEM(weight.shape, jnp.bfloat16),
            pltpu.VMEM((ticks, 2 * chunk, width), jnp.bfloat16),
            pltpu.VMEM((ticks, rows, depth), jnp.bfloat16),
            pltpu.VMEM((hops + 1, 2, groups, chunk, wide), jnp.bfloat16),
            pltpu.VMEM((2, 2, groups, chunk // 2, wide), jnp.bfloat16),
            pltpu.VMEM(residual.shape, jnp.bfloat16),
            pltpu.VMEM(residual.shape, jnp.float32),
            pltpu.SemaphoreType.DMA((4, 2)),
            pltpu.SemaphoreType.DMA((2, SPLIT)),
            pltpu.SemaphoreType.DMA((hops, 2, groups)),
            pltpu.SemaphoreType.DMA((hops, 2, groups)),
            pltpu.SemaphoreType.DMA((2, groups, 2)),
            pltpu.SemaphoreType.DMA((2, groups, 2)),
            pltpu.SemaphoreType.DMA((2,)),
        ],
        compiler_params=pltpu.CompilerParams(collective_id=0, has_side_effects=True, vmem_limit_bytes=24 * 1024 * 1024),
        name="attend_reduce_shift",
    )(
        *(
            pltpu.with_memory_space_constraint(a, pltpu.HBM)
            for a in (lengths, queries, new_kv, cache_kv, weight, residual)
        ),
    )
    return pl.pallas_call(
        hand_over_kernel,
        out_shape=jax.ShapeDtypeStruct(residual.shape, jnp.bfloat16),
        in_specs=[any_space],
        out_specs=any_space,
        scratch_shapes=[pltpu.SemaphoreType.DMA],
        compiler_params=pltpu.CompilerParams(vmem_limit_bytes=1024 * 1024),
        name="hand_over",
    )(result)


def solution(mesh):
    placed = (
        P(("section", "head"), None, None),
        P(None, "section", "head"),
        P(None, None, "section", None),
        P(None, "section", None),
        P(),
        P("section", "head", None),
    )
    return jax.shard_map(
        on_device,
        mesh=mesh,
        in_specs=placed,
        out_specs=P(("section", "head"), None, None),
        check_vma=False,
    )
```

```python
import functools
import math

import jax
import jax.numpy as jnp
from jax import lax
from jax.experimental import pallas as pl
from jax.experimental.pallas import tpu as pltpu
from jax.sharding import PartitionSpec as P

HD = 128
NEG = -1e30
SCALE = math.log2(math.e) / math.sqrt(HD)
SPLIT = 4
LAG = 3
SKEW = (0,) * SPLIT + (LAG,) * (SPLIT // 2) + (LAG + 1,) * (SPLIT // 2)
MESH = pl.DeviceIdType.MESH


def reduce_kernel(
    sections,
    heads_count,
    len_ref,
    q_hbm,
    new_ref,
    cache_ref,
    w_hbm,
    res_ref,
    out_ref,
    q_ref,
    kv,
    w_ref,
    mixed,
    part,
    buf,
    land,
    moved,
    summed,
    isem,
    wsem,
    ssem,
    rsem,
    zssem,
    zrsem,
    xsem,
):
    ny = heads_count // 2
    hops = ny - 1
    pairs = ny // 2
    groups = buf.shape[2]
    ticks, rows, width = q_ref.shape
    here = width // HD
    chunk = buf.shape[3]
    wide = buf.shape[4]
    own = chunk // 2
    half = w_ref.shape[1] // 2
    cached = cache_ref.shape[1]
    section = lax.axis_index("section")
    head = lax.axis_index("head")
    y = head // 2
    z = head % 2
    after = lax.rem(section + 1, sections)
    prior = lax.rem(section + sections - 1, sections)
    ring = (lax.rem(head + 2, heads_count), lax.rem(head + heads_count - 2, heads_count))
    column = pl.multiple_of((head // 2) * HD, HD)

    def column_of(d, g):
        return d * half + (g % SPLIT) * wide

    def w_copy(d, g):
        at = column_of(d, g)
        return pltpu.make_async_copy(
            w_hbm.at[:, at:at + wide], w_ref.at[:, at:at + wide], wsem.at[d, g]
        )

    def fresh_copy(t, i):
        at = t * (rows + cached)
        return pltpu.make_async_copy(
            new_ref.at[t, i, :, pl.ds(column, HD)],
            kv.at[i, at:at + rows, :],
            isem.at[1 + t, i],
        )

    def cache_copy(i):
        return pltpu.make_async_copy(
            cache_ref.at[i, :, pl.ds(column, HD)],
            kv.at[i, rows:rows + cached, :],
            isem.at[3, i],
        )

    q_copy = pltpu.make_async_copy(q_hbm, q_ref, isem.at[0, 0])
    q_copy.start()
    for i in range(2):
        fresh_copy(0, i).start()
        cache_copy(i).start()
    for g in range(SPLIT):
        for d in range(2):
            w_copy(d, g).start()
    for i in range(2):
        fresh_copy(1, i).start()

    barrier = pltpu.get_barrier_semaphore()
    for near in ring:
        pl.semaphore_signal(barrier, inc=1, device_id=(section, near), device_id_type=MESH)
    for other in range(2):
        for where in (after, prior):
            pl.semaphore_signal(
                barrier, inc=1, device_id=(where, 2 * y + other), device_id_type=MESH
            )

    def chunk_at(d, step):
        if d == 0:
            return lax.rem(y + 2 * ny - 1 - step, ny)
        return lax.rem(y + 1 + step, ny)

    def rows_of(c):
        return pl.ds(pl.multiple_of(c * chunk, chunk), chunk)

    def ring_copy(step, d, g):
        return pltpu.make_async_remote_copy(
            src_ref=buf.at[step, d, g],
            dst_ref=buf.at[step + 1, d, g],
            send_sem=ssem.at[step, d, g],
            recv_sem=rsem.at[step, d, g],
            device_id=(section, ring[d]),
            device_id_type=MESH,
        )

    def out_copy(d, g, target, source):
        return pltpu.make_async_remote_copy(
            src_ref=buf.at[hops, d, g, pl.ds(target * own, own), :],
            dst_ref=land.at[source, d, g],
            send_sem=zssem.at[d, g, target],
            recv_sem=zrsem.at[d, g, source],
            device_id=(after, 2 * y + target),
            device_id_type=MESH,
        )

    length = len_ref[section]

    def pair_of(p):
        return chunk_at(0, p), jnp.where(p == pairs - 1, y, chunk_at(1, p))

    def attend(t, p, before_values=None):
        pair = pair_of(p)
        q = jnp.concatenate(
            [q_ref[t, rows_of(c), h * HD:(h + 1) * HD] for h in range(here) for c in pair], axis=0
        )
        base = lax.broadcasted_iota(jnp.int32, (chunk, 1), 0)
        place = jnp.concatenate([base + c * chunk for h in range(here) for c in pair], axis=0)

        def scores(first, count):
            return lax.dot_general(
                q,
                kv[0, first:first + count, :],
                (((1,), (1,)), ((), ())),
                preferred_element_type=jnp.float32,
            )

        local = lax.broadcasted_iota(jnp.int32, (chunk * 2 * here, rows), 1)
        held = lax.broadcasted_iota(jnp.int32, (1, cached), 1)
        blocks = []
        first_block = scores(0, rows)
        blocks.append(jnp.where(local <= place, first_block, NEG) if t == 0 else first_block)
        blocks.append(jnp.where(held < length, scores(rows, cached), NEG))
        if t == 1:
            blocks.append(jnp.where(local <= place, scores(rows + cached, rows), NEG))
        s = jnp.concatenate(blocks, axis=1)
        m = jnp.max(s, axis=1, keepdims=True)
        w = jnp.exp2((s - m) * SCALE)
        total = jnp.sum(w, axis=1, keepdims=True)
        if before_values is not None:
            before_values()
        o = jnp.dot(
            w.astype(jnp.bfloat16), kv[1, 0:s.shape[1], :], preferred_element_type=jnp.float32
        )
        o = (o / total).astype(jnp.bfloat16)
        for h in range(here):
            mixed[t, :, h * HD:(h + 1) * HD] = o[2 * chunk * h:2 * chunk * (h + 1)]

    def project(t, p, d, g):
        pair = pair_of(p)
        at = column_of(d, g)
        block = jnp.dot(
            mixed[t], w_ref[:, at:at + wide], preferred_element_type=jnp.float32
        ).astype(jnp.bfloat16)
        for i in range(2):
            part[t, rows_of(pair[i]), at:at + wide] = block[i * chunk:(i + 1) * chunk]
        return block

    def values_here():
        fresh_copy(0, 1).wait()
        cache_copy(1).wait()

    q_copy.wait()
    fresh_copy(0, 0).wait()
    cache_copy(0).wait()
    attend(0, 0, values_here)
    for g in range(SPLIT):
        for d in range(2):
            w_copy(d, g).wait()
            buf[0, d, g] = project(0, 0, d, g)[d * chunk:(d + 1) * chunk]
        if g == 0:
            pl.semaphore_wait(barrier, 6)
        for d in range(2):
            ring_copy(0, d, g).start()
    res_copy = pltpu.make_async_remote_copy(
        src_ref=res_ref,
        dst_ref=moved,
        send_sem=xsem.at[0],
        recv_sem=xsem.at[1],
        device_id=(after, head),
        device_id_type=MESH,
    )
    res_copy.start()
    for i in range(2):
        fresh_copy(1, i).wait()

    def attend_next(k):
        for t in range(ticks):
            @pl.when(jnp.logical_and(k >= t * LAG, k < t * LAG + pairs))
            def _(t=t):
                attend(t, k - t * LAG)

    def project_next(k, d):
        for t in range(ticks):
            @pl.when(jnp.logical_and(k >= t * LAG, k < t * LAG + pairs))
            def _(t=t):
                for g in range(SPLIT):
                    project(t, k - t * LAG, d, g)

    attend_next(1)
    for d in range(2):
        project_next(1, d)

    def slot(now, carry):
        for g in range(SPLIT, groups):
            @pl.when(now == SKEW[g])
            def _(g=g):
                for d in range(2):
                    at = column_of(d, g)
                    buf[0, d, g] = part[1, rows_of(chunk_at(d, 0)), at:at + wide]
                    ring_copy(0, d, g).start()

        for g in range(groups):
            t = g // SPLIT
            step = now - SKEW[g]

            @pl.when(jnp.logical_and(step >= 1, step <= hops))
            def _(g=g, t=t, step=step):
                for d in range(2):
                    ring_copy(step - 1, d, g).wait_recv()
                    at = column_of(d, g)
                    mine = part[t, rows_of(chunk_at(d, step)), at:at + wide]
                    buf[step, d, g] = (
                        buf[step, d, g].astype(jnp.float32) + mine.astype(jnp.float32)
                    ).astype(jnp.bfloat16)

                    @pl.when(step < hops)
                    def _():
                        ring_copy(step, d, g).start()

                    @pl.when(step == hops)
                    def _():
                        for target in range(2):
                            out_copy(d, g, target, z).start()

            if g == SPLIT // 4:
                attend_next(now + 1)
            if g == SPLIT // 2:
                project_next(now + 1, 0)
            if g == SPLIT - 1:
                project_next(now + 1, 1)

        return carry

    lax.fori_loop(1, hops + 1 + max(SKEW), slot, 0)

    res_copy.wait_recv()
    for g in range(groups):
        for d in range(2):
            for other in range(2):
                out_copy(d, g, other, other).wait_recv()
            at = column_of(d, g)
            summed[:, g // SPLIT, at:at + wide] = land[0, d, g].astype(jnp.float32) + land[
                1, d, g
            ].astype(jnp.float32)
            if g >= groups - SPLIT:
                out_ref[:, :, at:at + wide] = (
                    summed[:, :, at:at + wide] + moved[:, :, at:at + wide].astype(jnp.float32)
                ).astype(jnp.bfloat16)
    for d in range(2):
        for g in range(groups):
            for other in range(2):
                out_copy(d, g, other, other).wait_send()

            def drain(step, carry, d=d, g=g):
                ring_copy(step, d, g).wait_send()
                return carry

            lax.fori_loop(0, hops, drain, 0)
    res_copy.wait_send()


def hand_over_kernel(in_ref, out_ref, sem):
    copy = pltpu.make_async_copy(in_ref, out_ref, sem)
    copy.start()
    copy.wait()


def on_device(residual, queries, new_kv, cache_kv, lengths, out_weight):
    sections = lax.axis_size("section")
    heads_count = lax.axis_size("head")
    weight = out_weight[0]
    ticks, rows, width = queries.shape
    depth = weight.shape[1]
    ny = heads_count // 2
    hops = ny - 1
    groups = ticks * SPLIT
    chunk = rows // ny
    wide = depth // 2 // SPLIT
    keys = cache_kv.shape[1] + ticks * rows
    any_space = pl.BlockSpec(memory_space=pl.ANY)
    result = pl.pallas_call(
        functools.partial(reduce_kernel, sections, heads_count),
        out_shape=jax.ShapeDtypeStruct(residual.shape, jnp.bfloat16),
        in_specs=[pl.BlockSpec(memory_space=pltpu.SMEM)]
        + [pl.BlockSpec(memory_space=pltpu.HBM)] * 5,
        out_specs=pl.BlockSpec(memory_space=pltpu.VMEM),
        scratch_shapes=[
            pltpu.VMEM((ticks, rows, width), jnp.bfloat16),
            pltpu.VMEM((2, keys, HD), jnp.bfloat16),
            pltpu.VMEM(weight.shape, jnp.bfloat16),
            pltpu.VMEM((ticks, 2 * chunk, width), jnp.bfloat16),
            pltpu.VMEM((ticks, rows, depth), jnp.bfloat16),
            pltpu.VMEM((hops + 1, 2, groups, chunk, wide), jnp.bfloat16),
            pltpu.VMEM((2, 2, groups, chunk // 2, wide), jnp.bfloat16),
            pltpu.VMEM(residual.shape, jnp.bfloat16),
            pltpu.VMEM(residual.shape, jnp.float32),
            pltpu.SemaphoreType.DMA((4, 2)),
            pltpu.SemaphoreType.DMA((2, SPLIT)),
            pltpu.SemaphoreType.DMA((hops, 2, groups)),
            pltpu.SemaphoreType.DMA((hops, 2, groups)),
            pltpu.SemaphoreType.DMA((2, groups, 2)),
            pltpu.SemaphoreType.DMA((2, groups, 2)),
            pltpu.SemaphoreType.DMA((2,)),
        ],
        compiler_params=pltpu.CompilerParams(collective_id=0, has_side_effects=True, vmem_limit_bytes=24 * 1024 * 1024),
        name="attend_reduce_shift",
    )(
        *(
            pltpu.with_memory_space_constraint(a, pltpu.HBM)
            for a in (lengths, queries, new_kv, cache_kv, weight, residual)
        ),
    )
    return pl.pallas_call(
        hand_over_kernel,
        out_shape=jax.ShapeDtypeStruct(residual.shape, jnp.bfloat16),
        in_specs=[any_space],
        out_specs=any_space,
        scratch_shapes=[pltpu.SemaphoreType.DMA],
        compiler_params=pltpu.CompilerParams(vmem_limit_bytes=1024 * 1024),
        name="hand_over",
    )(result)


def solution(mesh):
    placed = (
        P(("section", "head"), None, None),
        P(None, "section", "head"),
        P(None, None, "section", None),
        P(None, "section", None),
        P(),
        P("section", "head", None),
    )
    return jax.shard_map(
        on_device,
        mesh=mesh,
        in_specs=placed,
        out_specs=P(("section", "head"), None, None),
        check_vma=False,
    )
```
